32 devices in a mesh: blocks: 2 (over y), stripe: 4 (over z), cond: 2 (over x), col: 2 (over core).
Axes of the slice: x: 2, y: 2, z: 4, core: 2. Of those that a mesh axis runs over, the one named last changes fastest.
Arguments:
- theta: float32 [1024, 512], P(('blocks', 'stripe', 'cond'), 'col'), parts along dimension 0, may hold values from -6 to 6
- seed_map: int32 [1024, 512], P(('blocks', 'stripe', 'cond'), 'col'), parts along dimension 0, may hold values 0 or 1
- target: bfloat16 [1024, 512], P(('blocks', 'stripe'), 'col'), parts along dimension 0, may hold values from 0 to 1
- row_taps: bfloat16 [5, 6, 129], replicated, may hold values from -0.5 to 0.5
- col_taps: bfloat16 [5, 6, 129], replicated, may hold values from -0.5 to 0.5
- kernel_weight: float32 [5, 6], replicated, may hold values from 0.05 to 0.4
- cond_index: int32 [4], P('cond'), may hold values from 0 to 4
- dose: float32 [4], P('cond'), may hold values from 0.7 to 1.4
Outputs:
- grad_theta: float32 [1024, 512], P(('blocks', 'stripe', 'cond'), 'col'), parts along dimension 0
The draws below stay inside these ranges and needn't reach their ends.
There are 2 independent parts, one for each index of `blocks`. The reference program is written for one: setup_inputs(seed, part) draws one part's arguments, and reference() takes and returns one part's arrays. A program takes and returns all parts, laid end to end along the dimension named above; an argument that names none is the same for every part. Nothing has to cross between parts.
All inputs are finite; a program needn't handle non-finite values. No bound on the sum of `seed_map` on one device may be relied on, other than what follows from the above.
Results may differ from the reference program's by a relative error of at most 0.0059.
Values may be sent and summed in bfloat16 or wider, within the bound.
A program may use at most 64 MiB of HBM per device.

```python
import math
import jax
import jax.numpy as jnp
from jax import lax

HALF = 64
TAPS = 129
KERNELS = 6
FOCUS = 5
CONDS = 4
NR = 512
NC = 512


def touch_ends(values, rng, least, top_value):
    shape = values.shape
    place = [jax.random.randint(jax.random.fold_in(rng, axis), (), 0, shape[axis]) for axis in range(len(shape))]
    values = values.at[tuple(place)].set(least)
    longest = shape.index(max(shape))
    place[longest] = (place[longest] + 1) % shape[longest]
    return values.at[tuple(place)].set(top_value)


def steps_of(own_key, dims, split, least, top_value):
    gain = 1.0
    for axis_at, parts in split:
        steps = jax.random.uniform(jax.random.fold_in(jax.random.fold_in(own_key, 6), axis_at), (parts,), jnp.float32, least / len(split), top_value / len(split))
        gain = gain * jnp.repeat(jnp.exp(steps), dims[axis_at] // parts).reshape((-1,) + (1,) * (len(dims) - 1 - axis_at))
    return gain


def bell_draw(rng, dims, spread, most, cuts=(), kind=jnp.bfloat16):
    result = spread * jax.random.normal(rng, dims, jnp.float32)
    if cuts:
        result = result * steps_of(rng, dims, cuts, -0.22, 0.18)
    return jnp.clip(result, -most, most).astype(kind)


def setup_inputs(seed: int = 0, part: int = 0) -> dict:
    key_of = jax.random.split(jax.random.key(seed), 9)
    part_splits = jax.random.split(jax.random.fold_in(key_of[8], part), 9)
    return {
        "theta": bell_draw(part_splits[0], (NR, NC), 1.5, 6.0, ((0, 8), (1, 2)), jnp.float32),
        "seed_map": touch_ends((jax.random.randint(part_splits[1], (NR, NC), 0, 3) < 1).astype(jnp.int32), jax.random.fold_in(part_splits[1], 1), 0, 1),
        "target": jnp.clip(1.0 * jax.random.uniform(part_splits[2], (NR, NC), jnp.float32) ** steps_of(part_splits[2], (NR, NC), ((0, 4), (1, 2)), -0.2, 0.2), 0.0, 1.0).astype(jnp.bfloat16),
        "row_taps": bell_draw(key_of[3], (FOCUS, KERNELS, TAPS), TAPS ** -0.5, 0.5),
        "col_taps": bell_draw(key_of[4], (FOCUS, KERNELS, TAPS), TAPS ** -0.5, 0.5),
        "kernel_weight": jnp.clip(jnp.exp(jax.random.uniform(key_of[5], (FOCUS, KERNELS), jnp.float32, math.log(0.05), math.log(0.4))), 0.05, 0.4),
        "cond_index": touch_ends(jax.random.randint(key_of[6], (CONDS,), 0, FOCUS), jax.random.fold_in(key_of[6], 1), 0, FOCUS - 1).astype(jnp.int32),
        "dose": jnp.clip(jnp.exp(math.log(1.4) - 0.6931472 * jax.random.uniform(key_of[7], (CONDS,), jnp.float32) ** steps_of(key_of[7], (CONDS,), ((0, 2),), -0.2, 0.2)), 0.7, 1.4),
    }


seed_shift = 1.5
steepness = 4.0
threshold = 0.3


def correlate(values, kernel_array, padding_pairs, groups):
    return lax.conv_general_dilated(values, kernel_array, (1, 1), padding_pairs, feature_group_count=groups, precision=lax.Precision.HIGHEST)


def barrier_round(values):
    return lax.optimization_barrier(values.astype(jnp.bfloat16)).astype(jnp.float32)


def reference(theta, seed_map, target, row_taps, col_taps, kernel_weight, cond_index, dose):
    sig = jax.nn.sigmoid(theta + seed_shift * (2 * seed_map - 1).astype(jnp.float32))
    mask_value = barrier_round(sig)
    target_value = target.astype(jnp.float32)
    kernel_count = row_taps.shape[1]
    padded = jnp.pad(mask_value, ((0, 0), (HALF, HALF)))

    def one_condition(running, inputs):
        focus_row, dose_val = inputs
        row_tap = row_taps[focus_row].astype(jnp.float32)
        col_tap = col_taps[focus_row].astype(jnp.float32)
        weights = kernel_weight[focus_row]
        row_pass = correlate(padded[None, None], row_tap[:, None, :, None], ((HALF, HALF), (0, 0)), 1)
        row_pass = barrier_round(row_pass)
        field_amp = correlate(row_pass, col_tap[:, None, None, :], ((0, 0), (0, 0)), kernel_count)[0]
        intensity = jnp.sum(weights[:, None, None] * field_amp * field_amp, axis=0)
        resist = jax.nn.sigmoid(steepness * (dose_val * intensity - threshold))
        slope_term = 2.0 * (resist - target_value) * steepness * dose_val * resist * (1.0 - resist)
        dfield = barrier_round(2.0 * weights[:, None, None] * field_amp * slope_term[None])
        dpadded = jnp.pad(dfield, ((0, 0), (HALF, HALF), (0, 0)))
        col_back = correlate(dpadded[None], col_tap[:, ::-1][:, None, None, :], ((0, 0), (HALF, HALF)), kernel_count)
        col_back = barrier_round(col_back)
        grad_part = correlate(col_back, row_tap[:, ::-1][None, :, :, None], ((0, 0), (0, 0)), 1)[0, 0]
        return running + grad_part, None

    start = jnp.zeros(theta.shape, jnp.float32)
    grad_mask, unused = lax.scan(one_condition, start, (cond_index, dose))
    return grad_mask * sig * (1.0 - sig)
```

```python
import functools

import jax
import jax.numpy as jnp
from jax import lax
from jax.experimental import pallas as pl
from jax.experimental.pallas import tpu as pltpu
from jax.sharding import PartitionSpec as P

seed_shift = 1.5
steepness = 4.0
threshold = 0.3
f32 = jnp.float32
bf16 = jnp.bfloat16


def sigmoid(x):
    return 1.0 / (1.0 + jnp.exp(-x))


def toeplitz(row, count, shift):
    wide = jnp.broadcast_to(row, (count, row.shape[1]))
    return pltpu.roll(wide, shift, 1, stride=1, stride_axis=0)


def body(
    stripes,
    groups,
    cores,
    half,
    theta_ref,
    seed_ref,
    target_ref,
    row_taps_ref,
    col_taps_ref,
    weight_ref,
    cond_ref,
    dose_ref,
    out_ref,
    ext,
    tgt,
    sig_ref,
    taps_pad,
    fwd_rows,
    adj_rows,
    fwd_cols,
    adj_cols,
    row_pass,
    field,
    col_back,
    grad,
    grad_half,
    partial,
    send_m,
    recv_m,
    send_f,
    recv_f,
    send_t,
    recv_t,
    send_u,
    recv_u,
    send_g,
    recv_g,
):
    band = 2 * half
    rows, cols = theta_ref.shape
    stripe_rows = rows * groups
    wide = cols * cores
    kernels = row_taps_ref.shape[1]
    taps = row_taps_ref.shape[2]
    slots = cond_ref.shape[0] // cores
    stripe = lax.axis_index("stripe")
    group = lax.axis_index("cond")
    core = lax.axis_index("col")
    has_up = stripe > 0
    has_down = stripe < stripes - 1

    def when_block(block, fn):
        if block == 0:
            pl.when(has_up)(fn)
        elif block == 2:
            pl.when(has_down)(fn)
        else:
            fn()

    def peer(stripe_step, group_step, core_step):
        return {
            "stripe": stripe + stripe_step,
            "cond": lax.rem(group + group_step, groups),
            "col": lax.rem(core + core_step, cores),
        }

    barrier = pltpu.get_barrier_semaphore()

    def greet(stripe_step, group_step, core_step):
        pl.semaphore_signal(
            barrier,
            inc=1,
            device_id=peer(stripe_step, group_step, core_step),
            device_id_type=pl.DeviceIdType.MESH,
        )

    for group_step in range(groups):
        for core_step in range(cores):
            if group_step or core_step:
                greet(0, group_step, core_step)

    for block in (0, 2):

        def greet_block(block=block):
            for group_step in range(groups):
                greet(block - 1, group_step, 0)

        when_block(block, greet_block)

    sig = sigmoid(theta_ref[...] + seed_shift * (2 * seed_ref[...] - 1).astype(f32))
    sig_ref[...] = sig

    def window(block, source_group, source_core):
        first = pl.multiple_of(block * stripe_rows + source_group * rows, rows)
        left = pl.multiple_of(source_core * cols, cols)
        return ext.at[pl.ds(first, rows), pl.ds(left, cols)]

    own_first = pl.multiple_of(stripe_rows + group * rows, rows)
    own_left = pl.multiple_of(core * cols, cols)
    ext[pl.ds(own_first, rows), pl.ds(own_left, cols)] = sig.astype(bf16)

    neighbours = jnp.where(has_up, groups, 0) + jnp.where(has_down, groups, 0)
    pl.semaphore_wait(barrier, groups * cores - 1 + neighbours)

    def mask_copy(block, group_step):
        first = pl.multiple_of((2 - block) * stripe_rows + group * rows, rows)
        return pltpu.make_async_remote_copy(
            src_ref=window(1, group, core),
            dst_ref=ext.at[pl.ds(first, rows), pl.ds(own_left, cols)],
            send_sem=send_m.at[block, group_step],
            recv_sem=recv_m.at[2 - block, group_step],
            device_id=peer(block - 1, group_step, 0),
            device_id_type=pl.DeviceIdType.MESH,
        )

    def forward(block, group_step):
        source = lax.rem(group - group_step + groups, groups)
        tile = window(block, source, core)
        return pltpu.make_async_remote_copy(
            src_ref=tile,
            dst_ref=tile,
            send_sem=send_f.at[block, group_step],
            recv_sem=recv_f.at[block, group_step],
            device_id=peer(0, 0, 1),
            device_id_type=pl.DeviceIdType.MESH,
        )

    def mask_arrival(block, group_step):
        source = lax.rem(group - group_step + groups, groups)
        tile = window(block, source, core)
        return pltpu.make_async_remote_copy(
            src_ref=tile,
            dst_ref=tile,
            send_sem=send_m.at[block, group_step],
            recv_sem=recv_m.at[block, group_step],
            device_id=peer(0, 0, 1),
            device_id_type=pl.DeviceIdType.MESH,
        )

    def forward_arrival(block, group_step):
        source = lax.rem(group - group_step + groups, groups)
        tile = window(block, source, 1 - core)
        return pltpu.make_async_remote_copy(
            src_ref=tile,
            dst_ref=tile,
            send_sem=send_f.at[block, group_step],
            recv_sem=recv_f.at[block, group_step],
            device_id=peer(0, 0, 1),
            device_id_type=pl.DeviceIdType.MESH,
        )

    def target_rows(block):
        if block == 0:
            return pl.ds(0, half)
        if block == 1:
            return pl.ds(half, stripe_rows)
        return pl.ds(half + stripe_rows, half)

    def target_copy(block):
        source = pl.ds(0, half) if block == 0 else pl.ds(stripe_rows - half, half)
        return pltpu.make_async_remote_copy(
            src_ref=target_ref.at[source, :],
            dst_ref=tgt.at[target_rows(2 - block), pl.ds(own_left, cols)],
            send_sem=send_t.at[block],
            recv_sem=recv_t.at[2 - block],
            device_id=peer(block - 1, 0, 0),
            device_id_type=pl.DeviceIdType.MESH,
        )

    other_left = pl.multiple_of((1 - core) * cols, cols)

    def target_move(block, left, first):
        tile = tgt.at[target_rows(block), pl.ds(left, cols)]
        return pltpu.make_async_remote_copy(
            src_ref=target_ref if first and block == 1 else tile,
            dst_ref=tile,
            send_sem=send_u.at[block],
            recv_sem=recv_u.at[block],
            device_id=peer(0, 0, 1),
            device_id_type=pl.DeviceIdType.MESH,
        )

    def target_arrival(block):
        tile = tgt.at[target_rows(block), pl.ds(own_left, cols)]
        return pltpu.make_async_remote_copy(
            src_ref=tile,
            dst_ref=tile,
            send_sem=send_t.at[block],
            recv_sem=recv_t.at[block],
            device_id=peer(0, 0, 1),
            device_id_type=pl.DeviceIdType.MESH,
        )

    steps = [(b, g) for g in range(groups) for b in (0, 2, 1)]
    remote_steps = [(b, g) for b, g in steps if (b, g) != (1, 0)]

    for block, group_step in reversed(remote_steps):
        when_block(block, lambda b=block, g=group_step: mask_copy(b, g).start())
    forward(1, 0).start()
    for block in (0, 2):
        when_block(block, lambda b=block: target_copy(b).start())
    target_move(1, own_left, True).start()
    tgt[target_rows(1), pl.ds(own_left, cols)] = target_ref[...]

    @pl.when(jnp.logical_not(has_up))
    def _():
        ext[pl.ds(0, stripe_rows), :] = jnp.zeros((stripe_rows, wide), bf16)
        tgt[target_rows(0), :] = jnp.zeros((half, wide), bf16)

    @pl.when(jnp.logical_not(has_down))
    def _():
        ext[pl.ds(2 * stripe_rows, stripe_rows), :] = jnp.zeros((stripe_rows, wide), bf16)
        tgt[target_rows(2), :] = jnp.zeros((half, wide), bf16)

    taps_pad[...] = jnp.zeros_like(taps_pad)
    mirror = (
        lax.broadcasted_iota(jnp.int32, (2 * band, 3 * band), 0)
        + lax.broadcasted_iota(jnp.int32, (2 * band, 3 * band), 1)
        == band
    ).astype(f32).astype(bf16)

    for slot in range(slots):
        place = core * slots + slot
        focus = cond_ref[place]
        dose = dose_ref[place]

        taps_pad[0, 0:kernels, 0:taps] = row_taps_ref[focus].astype(f32)
        taps_pad[1, 0:kernels, 0:taps] = col_taps_ref[focus].astype(f32)
        for which in range(2):
            taps_pad[2 + which] = jnp.dot(
                taps_pad[which, :, 0 : 2 * band].astype(bf16),
                mirror,
                preferred_element_type=f32,
            )
        for k in range(kernels):
            tile = pl.ds(k * band, band)
            fwd_rows[tile, :] = toeplitz(taps_pad[0, k : k + 1, 0 : 2 * band], band, 0).astype(bf16)
            adjoint = toeplitz(taps_pad[2, k : k + 1, 0 : 2 * band], band, 0).astype(bf16)
            adj_rows[:, tile] = adjoint[:, :band]
            adj_rows[:, pl.ds((kernels + k) * band, band)] = adjoint[:, band:]
            for matrix, which in ((fwd_cols, 3), (adj_cols, 1)):
                strip = toeplitz(taps_pad[which, k : k + 1, :], band, half).astype(bf16)
                matrix[k, 0:band, 0:band] = strip[:, 2 * band :]
                matrix[k, 0:band, band:] = jnp.zeros((band, band), bf16)
                matrix[k, band : 2 * band, :] = strip[:, band:]
                matrix[k, 2 * band : 3 * band, :] = strip[:, : 2 * band]
                matrix[k, 3 * band :, 0:band] = jnp.zeros((band, band), bf16)
                matrix[k, 3 * band :, band:] = strip[:, 0:band]

        if slot == 0:
            for block, group_step in remote_steps:

                def relay(b=block, g=group_step):
                    mask_arrival(b, g).wait_recv()
                    forward(b, g).start()

                when_block(block, relay)
            for block in (0, 2):

                def relay_target(b=block):
                    target_arrival(b).wait_recv()
                    target_move(b, own_left, False).start()

                when_block(block, relay_target)
            for block, group_step in steps:
                when_block(block, lambda b=block, g=group_step: forward_arrival(b, g).wait_recv())

        def banded(left_side, matrix):
            span = 3 * band
            pieces = []
            for first in range(0, wide, 2 * band):
                low = max(first - band, 0)
                high = min(first + 3 * band, wide)
                top = low - (first - band)
                pieces.append(
                    jnp.dot(
                        left_side[:, low:high],
                        matrix[top : top + high - low, :],
                        preferred_element_type=f32,
                    )
                )
            return jnp.concatenate(pieces, axis=1)

        for part in range(2):
            row_pass[...] = jnp.dot(
                fwd_rows[...],
                ext[part * band : (part + 2) * band, :],
                preferred_element_type=f32,
            ).astype(bf16)
            intensity = jnp.zeros((band, wide), f32)
            for k in range(kernels):
                amp = banded(row_pass[k * band : (k + 1) * band, :], fwd_cols[k])
                field[k] = amp
                intensity = intensity + weight_ref[focus, k] * (amp * amp)
            if slot == 0 and part == 0:
                for block in (0, 1, 2):
                    when_block(
                        block, lambda b=block: target_move(b, other_left, False).wait_recv()
                    )
            resist = sigmoid(steepness * (dose * intensity - threshold))
            aim = tgt[part * band : (part + 1) * band, :].astype(f32)
            row_at = (
                stripe * stripe_rows
                + (part * band - half)
                + lax.broadcasted_iota(jnp.int32, (band, wide), 0)
            )
            inside = (row_at >= 0) & (row_at < stripes * stripe_rows)
            slope = (2.0 * steepness) * (resist - aim) * dose * resist * (1.0 - resist)
            slope = jnp.where(inside, slope, 0.0)
            for k in range(kernels):
                dfield = ((2.0 * weight_ref[focus, k]) * field[k] * slope).astype(bf16)
                col_back[pl.ds((part * kernels + k) * band, band), :] = banded(
                    dfield, adj_cols[k]
                ).astype(bf16)
        total = jnp.dot(adj_rows[...], col_back[...], preferred_element_type=f32)
        if slot == 0:
            grad[...] = total
        else:
            grad[...] += total

    grad_half[...] = grad[...].astype(bf16)

    def grad_copy(group_step, core_step):
        to = peer(0, group_step, core_step)
        place = group_step * cores + core_step - 1
        return pltpu.make_async_remote_copy(
            src_ref=grad_half.at[
                pl.ds(pl.multiple_of(to["cond"] * rows, rows), rows),
                pl.ds(pl.multiple_of(to["col"] * cols, cols), cols),
            ],
            dst_ref=partial.at[place],
            send_sem=send_g.at[place],
            recv_sem=recv_g.at[place],
            device_id=to,
            device_id_type=pl.DeviceIdType.MESH,
        )

    others = [(g, c) for g in range(groups) for c in range(cores) if g or c]
    for group_step, core_step in reversed(others):
        grad_copy(group_step, core_step).start()
    mine = grad[pl.ds(pl.multiple_of(group * rows, rows), rows), pl.ds(own_left, cols)]
    for group_step, core_step in others:
        grad_copy(group_step, core_step).wait_recv()
        mine = mine + partial[group_step * cores + core_step - 1].astype(f32)
    sig = sig_ref[...]
    out_ref[...] = mine * sig * (1.0 - sig)

    for block, group_step in remote_steps:
        def settle(b=block, g=group_step):
            mask_copy(b, g).wait_send()
            forward(b, g).wait_send()

        when_block(block, settle)
    forward(1, 0).wait_send()
    for block in (0, 2):
        def settle_target(b=block):
            target_copy(b).wait_send()
            target_move(b, own_left, False).wait_send()

        when_block(block, settle_target)
    target_move(1, own_left, True).wait_send()
    for group_step, core_step in others:
        grad_copy(group_step, core_step).wait_send()


def shards(stripes, groups, cores, theta, seed_map, target, row_taps, col_taps, weight, cond_index, dose):
    rows, cols = theta.shape
    kernels, taps = row_taps.shape[1:]
    half = taps // 2
    band = 2 * half
    stripe_rows = rows * groups
    wide = cols * cores
    tall = stripe_rows + 2 * band
    vmem = pl.BlockSpec(memory_space=pltpu.VMEM)
    smem = pl.BlockSpec(memory_space=pltpu.SMEM)
    dma = pltpu.SemaphoreType.DMA
    peers = groups * cores - 1
    return pl.pallas_call(
        functools.partial(body, stripes, groups, cores, half),
        out_shape=jax.ShapeDtypeStruct((rows, cols), f32),
        in_specs=[vmem, vmem, vmem, vmem, vmem, smem, smem, smem],
        out_specs=vmem,
        scratch_shapes=[
            pltpu.VMEM((tall, wide), bf16),
            pltpu.VMEM((stripe_rows + band, wide), bf16),
            pltpu.VMEM((rows, cols), f32),
            pltpu.VMEM((4, 8, 3 * band), f32),
            pltpu.VMEM((kernels * band, 2 * band), bf16),
            pltpu.VMEM((band, 2 * kernels * band), bf16),
            pltpu.VMEM((kernels, 4 * band, 2 * band), bf16),
            pltpu.VMEM((kernels, 4 * band, 2 * band), bf16),
            pltpu.VMEM((kernels * band, wide), bf16),
            pltpu.VMEM((kernels, band, wide), f32),
            pltpu.VMEM((2 * kernels * band, wide), bf16),
            pltpu.VMEM((stripe_rows, wide), f32),
            pltpu.VMEM((stripe_rows, wide), bf16),
            pltpu.VMEM((peers, rows, cols), bf16),
            dma((3, groups)),
            dma((3, groups)),
            dma((3, groups)),
            dma((3, groups)),
            dma((3,)),
            dma((3,)),
            dma((3,)),
            dma((3,)),
            dma((peers,)),
            dma((peers,)),
        ],
        compiler_params=pltpu.CompilerParams(
            collective_id=0, has_side_effects=True, vmem_limit_bytes=40 * 1024 * 1024
        ),
    )(theta, seed_map, target, row_taps, col_taps, weight, cond_index, dose)


def solution(mesh):
    sizes = [mesh.shape[name] for name in ("stripe", "cond", "col")]
    return jax.shard_map(
        functools.partial(shards, *sizes),
        mesh=mesh,
        in_specs=(
            P(("blocks", "stripe", "cond"), "col"),
            P(("blocks", "stripe", "cond"), "col"),
            P(("blocks", "stripe"), "col"),
            P(),
            P(),
            P(),
            P("cond"),
            P("cond"),
        ),
        out_specs=P(("blocks", "stripe", "cond"), "col"),
        check_vma=False,
    )
```

```python
import functools

import jax
import jax.numpy as jnp
from jax import lax
from jax.experimental import pallas as pl
from jax.experimental.pallas import tpu as pltpu
from jax.sharding import PartitionSpec as P

seed_shift = 1.5
steepness = 4.0
threshold = 0.3
f32 = jnp.float32
bf16 = jnp.bfloat16


def sigmoid(x):
    return 1.0 / (1.0 + jnp.exp(-x))


def toeplitz(row, count, shift):
    wide = jnp.broadcast_to(row, (count, row.shape[1]))
    return pltpu.roll(wide, shift, 1, stride=1, stride_axis=0)


def body(
    stripes,
    groups,
    cores,
    half,
    theta_in,
    seed_in,
    target_in,
    row_taps_in,
    col_taps_in,
    weight_in,
    cond_in,
    dose_in,
    out_ref,
    theta_ref,
    seed_ref,
    target_ref,
    row_taps_ref,
    col_taps_ref,
    weight_ref,
    cond_ref,
    dose_ref,
    load_sem,
    ext,
    tgt,
    sig_ref,
    taps_pad,
    fwd_rows,
    adj_rows,
    fwd_cols,
    adj_cols,
    row_pass,
    field,
    col_back,
    grad,
    grad_half,
    partial,
    send_m,
    recv_m,
    send_f,
    recv_f,
    send_t,
    recv_t,
    send_u,
    recv_u,
    send_g,
    recv_g,
):
    band = 2 * half
    rows, cols = theta_ref.shape
    stripe_rows = rows * groups
    wide = cols * cores
    kernels = row_taps_ref.shape[1]
    taps = row_taps_ref.shape[2]
    slots = cond_ref.shape[0] // cores
    stripe = lax.axis_index("stripe")
    group = lax.axis_index("cond")
    core = lax.axis_index("col")
    has_up = stripe > 0
    has_down = stripe < stripes - 1

    def when_block(block, fn):
        if block == 0:
            pl.when(has_up)(fn)
        elif block == 2:
            pl.when(has_down)(fn)
        else:
            fn()

    def peer(stripe_step, group_step, core_step):
        return {
            "stripe": stripe + stripe_step,
            "cond": lax.rem(group + group_step, groups),
            "col": lax.rem(core + core_step, cores),
        }

    pairs = (
        (theta_in, theta_ref),
        (seed_in, seed_ref),
        (target_in, target_ref),
        (row_taps_in, row_taps_ref),
        (col_taps_in, col_taps_ref),
        (weight_in, weight_ref),
        (cond_in, cond_ref),
        (dose_in, dose_ref),
    )
    loads = [
        pltpu.make_async_copy(source, into, load_sem.at[i])
        for i, (source, into) in enumerate(pairs)
    ]
    for load in loads:
        load.start()

    barrier = pltpu.get_barrier_semaphore()

    def greet(stripe_step, group_step, core_step):
        pl.semaphore_signal(
            barrier,
            inc=1,
            device_id=peer(stripe_step, group_step, core_step),
            device_id_type=pl.DeviceIdType.MESH,
        )

    for group_step in range(groups):
        for core_step in range(cores):
            if group_step or core_step:
                greet(0, group_step, core_step)

    for block in (0, 2):

        def greet_block(block=block):
            for group_step in range(groups):
                greet(block - 1, group_step, 0)

        when_block(block, greet_block)

    loads[0].wait()
    loads[1].wait()
    sig = sigmoid(theta_ref[...] + seed_shift * (2 * seed_ref[...] - 1).astype(f32))
    sig_ref[...] = sig

    def window(block, source_group, source_core):
        first = pl.multiple_of(block * stripe_rows + source_group * rows, rows)
        left = pl.multiple_of(source_core * cols, cols)
        return ext.at[pl.ds(first, rows), pl.ds(left, cols)]

    own_first = pl.multiple_of(stripe_rows + group * rows, rows)
    own_left = pl.multiple_of(core * cols, cols)
    ext[pl.ds(own_first, rows), pl.ds(own_left, cols)] = sig.astype(bf16)

    neighbours = jnp.where(has_up, groups, 0) + jnp.where(has_down, groups, 0)
    pl.semaphore_wait(barrier, groups * cores - 1 + neighbours)

    def mask_copy(block, group_step):
        first = pl.multiple_of((2 - block) * stripe_rows + group * rows, rows)
        return pltpu.make_async_remote_copy(
            src_ref=window(1, group, core),
            dst_ref=ext.at[pl.ds(first, rows), pl.ds(own_left, cols)],
            send_sem=send_m.at[block, group_step],
            recv_sem=recv_m.at[2 - block, group_step],
            device_id=peer(block - 1, group_step, 0),
            device_id_type=pl.DeviceIdType.MESH,
        )

    def forward(block, group_step):
        source = lax.rem(group - group_step + groups, groups)
        tile = window(block, source, core)
        return pltpu.make_async_remote_copy(
            src_ref=tile,
            dst_ref=tile,
            send_sem=send_f.at[block, group_step],
            recv_sem=recv_f.at[block, group_step],
            device_id=peer(0, 0, 1),
            device_id_type=pl.DeviceIdType.MESH,
        )

    def mask_arrival(block, group_step):
        source = lax.rem(group - group_step + groups, groups)
        tile = window(block, source, core)
        return pltpu.make_async_remote_copy(
            src_ref=tile,
            dst_ref=tile,
            send_sem=send_m.at[block, group_step],
            recv_sem=recv_m.at[block, group_step],
            device_id=peer(0, 0, 1),
            device_id_type=pl.DeviceIdType.MESH,
        )

    def forward_arrival(block, group_step):
        source = lax.rem(group - group_step + groups, groups)
        tile = window(block, source, 1 - core)
        return pltpu.make_async_remote_copy(
            src_ref=tile,
            dst_ref=tile,
            send_sem=send_f.at[block, group_step],
            recv_sem=recv_f.at[block, group_step],
            device_id=peer(0, 0, 1),
            device_id_type=pl.DeviceIdType.MESH,
        )

    def target_rows(block):
        if block == 0:
            return pl.ds(0, half)
        if block == 1:
            return pl.ds(half, stripe_rows)
        return pl.ds(half + stripe_rows, half)

    def target_copy(block):
        source = pl.ds(0, half) if block == 0 else pl.ds(stripe_rows - half, half)
        return pltpu.make_async_remote_copy(
            src_ref=target_ref.at[source, :],
            dst_ref=tgt.at[target_rows(2 - block), pl.ds(own_left, cols)],
            send_sem=send_t.at[block],
            recv_sem=recv_t.at[2 - block],
            device_id=peer(block - 1, 0, 0),
            device_id_type=pl.DeviceIdType.MESH,
        )

    other_left = pl.multiple_of((1 - core) * cols, cols)

    def target_move(block, left, first):
        tile = tgt.at[target_rows(block), pl.ds(left, cols)]
        return pltpu.make_async_remote_copy(
            src_ref=target_ref if first and block == 1 else tile,
            dst_ref=tile,
            send_sem=send_u.at[block],
            recv_sem=recv_u.at[block],
            device_id=peer(0, 0, 1),
            device_id_type=pl.DeviceIdType.MESH,
        )

    def target_arrival(block):
        tile = tgt.at[target_rows(block), pl.ds(own_left, cols)]
        return pltpu.make_async_remote_copy(
            src_ref=tile,
            dst_ref=tile,
            send_sem=send_t.at[block],
            recv_sem=recv_t.at[block],
            device_id=peer(0, 0, 1),
            device_id_type=pl.DeviceIdType.MESH,
        )

    loads[2].wait()
    steps = [(b, g) for g in range(groups) for b in (0, 2, 1)]
    remote_steps = [(b, g) for b, g in steps if (b, g) != (1, 0)]

    for block, group_step in reversed(remote_steps):
        when_block(block, lambda b=block, g=group_step: mask_copy(b, g).start())
    forward(1, 0).start()
    for block in (0, 2):
        when_block(block, lambda b=block: target_copy(b).start())
    target_move(1, own_left, True).start()
    tgt[target_rows(1), pl.ds(own_left, cols)] = target_ref[...]

    @pl.when(jnp.logical_not(has_up))
    def _():
        ext[pl.ds(0, stripe_rows), :] = jnp.zeros((stripe_rows, wide), bf16)
        tgt[target_rows(0), :] = jnp.zeros((half, wide), bf16)

    @pl.when(jnp.logical_not(has_down))
    def _():
        ext[pl.ds(2 * stripe_rows, stripe_rows), :] = jnp.zeros((stripe_rows, wide), bf16)
        tgt[target_rows(2), :] = jnp.zeros((half, wide), bf16)

    taps_pad[...] = jnp.zeros_like(taps_pad)
    mirror = (
        lax.broadcasted_iota(jnp.int32, (2 * band, 3 * band), 0)
        + lax.broadcasted_iota(jnp.int32, (2 * band, 3 * band), 1)
        == band
    ).astype(f32).astype(bf16)

    for load in loads[3:]:
        load.wait()

    for slot in range(slots):
        place = core * slots + slot
        focus = cond_ref[place]
        dose = dose_ref[place]

        taps_pad[0, 0:kernels, 0:taps] = row_taps_ref[focus].astype(f32)
        taps_pad[1, 0:kernels, 0:taps] = col_taps_ref[focus].astype(f32)
        for which in range(2):
            taps_pad[2 + which] = jnp.dot(
                taps_pad[which, :, 0 : 2 * band].astype(bf16),
                mirror,
                preferred_element_type=f32,
            )
        for k in range(kernels):
            tile = pl.ds(k * band, band)
            fwd_rows[tile, :] = toeplitz(taps_pad[0, k : k + 1, 0 : 2 * band], band, 0).astype(bf16)
            adjoint = toeplitz(taps_pad[2, k : k + 1, 0 : 2 * band], band, 0).astype(bf16)
            adj_rows[:, tile] = adjoint[:, :band]
            adj_rows[:, pl.ds((kernels + k) * band, band)] = adjoint[:, band:]
            for matrix, which in ((fwd_cols, 3), (adj_cols, 1)):
                strip = toeplitz(taps_pad[which, k : k + 1, :], band, half).astype(bf16)
                matrix[k, 0:band, 0:band] = strip[:, 2 * band :]
                matrix[k, 0:band, band:] = jnp.zeros((band, band), bf16)
                matrix[k, band : 2 * band, :] = strip[:, band:]
                matrix[k, 2 * band : 3 * band, :] = strip[:, : 2 * band]
                matrix[k, 3 * band :, 0:band] = jnp.zeros((band, band), bf16)
                matrix[k, 3 * band :, band:] = strip[:, 0:band]

        if slot == 0:
            for block, group_step in remote_steps:

                def relay(b=block, g=group_step):
                    mask_arrival(b, g).wait_recv()
                    forward(b, g).start()

                when_block(block, relay)
            for block in (0, 2):

                def relay_target(b=block):
                    target_arrival(b).wait_recv()
                    target_move(b, own_left, False).start()

                when_block(block, relay_target)
            for block, group_step in steps:
                when_block(block, lambda b=block, g=group_step: forward_arrival(b, g).wait_recv())

        def banded(left_side, matrix):
            span = 3 * band
            pieces = []
            for first in range(0, wide, 2 * band):
                low = max(first - band, 0)
                high = min(first + 3 * band, wide)
                top = low - (first - band)
                pieces.append(
                    jnp.dot(
                        left_side[:, low:high],
                        matrix[top : top + high - low, :],
                        preferred_element_type=f32,
                    )
                )
            return jnp.concatenate(pieces, axis=1)

        for part in range(2):
            row_pass[...] = jnp.dot(
                fwd_rows[...],
                ext[part * band : (part + 2) * band, :],
                preferred_element_type=f32,
            ).astype(bf16)
            intensity = jnp.zeros((band, wide), f32)
            for k in range(kernels):
                amp = banded(row_pass[k * band : (k + 1) * band, :], fwd_cols[k])
                field[k] = amp
                intensity = intensity + weight_ref[focus, k] * (amp * amp)
            if slot == 0 and part == 0:
                for block in (0, 1, 2):
                    when_block(
                        block, lambda b=block: target_move(b, other_left, False).wait_recv()
                    )
            resist = sigmoid(steepness * (dose * intensity - threshold))
            aim = tgt[part * band : (part + 1) * band, :].astype(f32)
            row_at = (
                stripe * stripe_rows
                + (part * band - half)
                + lax.broadcasted_iota(jnp.int32, (band, wide), 0)
            )
            inside = (row_at >= 0) & (row_at < stripes * stripe_rows)
            slope = (2.0 * steepness) * (resist - aim) * dose * resist * (1.0 - resist)
            slope = jnp.where(inside, slope, 0.0)
            for k in range(kernels):
                dfield = ((2.0 * weight_ref[focus, k]) * field[k] * slope).astype(bf16)
                col_back[pl.ds((part * kernels + k) * band, band), :] = banded(
                    dfield, adj_cols[k]
                ).astype(bf16)
        total = jnp.dot(adj_rows[...], col_back[...], preferred_element_type=f32)
        if slot == 0:
            grad[...] = total
        else:
            grad[...] += total

    grad_half[...] = grad[...].astype(bf16)

    def grad_copy(group_step, core_step):
        to = peer(0, group_step, core_step)
        place = group_step * cores + core_step - 1
        return pltpu.make_async_remote_copy(
            src_ref=grad_half.at[
                pl.ds(pl.multiple_of(to["cond"] * rows, rows), rows),
                pl.ds(pl.multiple_of(to["col"] * cols, cols), cols),
            ],
            dst_ref=partial.at[place],
            send_sem=send_g.at[place],
            recv_sem=recv_g.at[place],
            device_id=to,
            device_id_type=pl.DeviceIdType.MESH,
        )

    others = [(g, c) for g in range(groups) for c in range(cores) if g or c]
    for group_step, core_step in reversed(others):
        grad_copy(group_step, core_step).start()
    mine = grad[pl.ds(pl.multiple_of(group * rows, rows), rows), pl.ds(own_left, cols)]
    for group_step, core_step in others:
        grad_copy(group_step, core_step).wait_recv()
        mine = mine + partial[group_step * cores + core_step - 1].astype(f32)
    sig = sig_ref[...]
    out_ref[...] = mine * sig * (1.0 - sig)

    for block, group_step in remote_steps:
        def settle(b=block, g=group_step):
            mask_copy(b, g).wait_send()
            forward(b, g).wait_send()

        when_block(block, settle)
    forward(1, 0).wait_send()
    for block in (0, 2):
        def settle_target(b=block):
            target_copy(b).wait_send()
            target_move(b, own_left, False).wait_send()

        when_block(block, settle_target)
    target_move(1, own_left, True).wait_send()
    for group_step, core_step in others:
        grad_copy(group_step, core_step).wait_send()


def shards(stripes, groups, cores, theta, seed_map, target, row_taps, col_taps, weight, cond_index, dose):
    rows, cols = theta.shape
    kernels, taps = row_taps.shape[1:]
    half = taps // 2
    band = 2 * half
    stripe_rows = rows * groups
    wide = cols * cores
    tall = stripe_rows + 2 * band
    vmem = pl.BlockSpec(memory_space=pltpu.VMEM)
    hbm = pl.BlockSpec(memory_space=pltpu.HBM)
    dma = pltpu.SemaphoreType.DMA
    peers = groups * cores - 1
    return pl.pallas_call(
        functools.partial(body, stripes, groups, cores, half),
        out_shape=jax.ShapeDtypeStruct((rows, cols), f32),
        in_specs=[hbm] * 8,
        out_specs=vmem,
        scratch_shapes=[
            *[pltpu.VMEM(a.shape, a.dtype) for a in (theta, seed_map, target, row_taps, col_taps)],
            *[pltpu.SMEM(a.shape, a.dtype) for a in (weight, cond_index, dose)],
            dma((8,)),
            pltpu.VMEM((tall, wide), bf16),
            pltpu.VMEM((stripe_rows + band, wide), bf16),
            pltpu.VMEM((rows, cols), f32),
            pltpu.VMEM((4, 8, 3 * band), f32),
            pltpu.VMEM((kernels * band, 2 * band), bf16),
            pltpu.VMEM((band, 2 * kernels * band), bf16),
            pltpu.VMEM((kernels, 4 * band, 2 * band), bf16),
            pltpu.VMEM((kernels, 4 * band, 2 * band), bf16),
            pltpu.VMEM((kernels * band, wide), bf16),
            pltpu.VMEM((kernels, band, wide), f32),
            pltpu.VMEM((2 * kernels * band, wide), bf16),
            pltpu.VMEM((stripe_rows, wide), f32),
            pltpu.VMEM((stripe_rows, wide), bf16),
            pltpu.VMEM((peers, rows, cols), bf16),
            dma((3, groups)),
            dma((3, groups)),
            dma((3, groups)),
            dma((3, groups)),
            dma((3,)),
            dma((3,)),
            dma((3,)),
            dma((3,)),
            dma((peers,)),
            dma((peers,)),
        ],
        compiler_params=pltpu.CompilerParams(
            collective_id=0, has_side_effects=True, vmem_limit_bytes=64 * 1024 * 1024
        ),
    )(theta, seed_map, target, row_taps, col_taps, weight, cond_index, dose)


def solution(mesh):
    sizes = [mesh.shape[name] for name in ("stripe", "cond", "col")]
    return jax.shard_map(
        functools.partial(shards, *sizes),
        mesh=mesh,
        in_specs=(
            P(("blocks", "stripe", "cond"), "col"),
            P(("blocks", "stripe", "cond"), "col"),
            P(("blocks", "stripe"), "col"),
            P(),
            P(),
            P(),
            P("cond"),
            P("cond"),
        ),
        out_specs=P(("blocks", "stripe", "cond"), "col"),
        check_vma=False,
    )
```

```python
import functools

import jax
import jax.numpy as jnp
from jax import lax
from jax.experimental import pallas as pl
from jax.experimental.pallas import tpu as pltpu
from jax.sharding import PartitionSpec as P

seed_shift = 1.5
steepness = 4.0
threshold = 0.3
f32 = jnp.float32
bf16 = jnp.bfloat16


def sigmoid(x):
    return 1.0 / (1.0 + jnp.exp(-x))


def toeplitz(row, count, shift):
    wide = jnp.broadcast_to(row, (count, row.shape[1]))
    return pltpu.roll(wide, shift, 1, stride=1, stride_axis=0)


def body(
    stripes,
    groups,
    cores,
    half,
    theta_in,
    seed_in,
    target_in,
    row_taps_in,
    col_taps_in,
    weight_in,
    cond_in,
    dose_in,
    out_ref,
    theta_ref,
    seed_ref,
    target_ref,
    row_taps_ref,
    col_taps_ref,
    weight_ref,
    cond_ref,
    dose_ref,
    load_sem,
    ext,
    tgt,
    sig_ref,
    taps_pad,
    fwd_rows,
    adj_rows,
    fwd_cols,
    adj_cols,
    row_pass,
    field,
    col_back,
    grad,
    grad_half,
    partial,
    partial_far,
    total_ref,
    send_m,
    recv_m,
    send_f,
    recv_f,
    send_t,
    recv_t,
    send_g,
    recv_g,
    send_h,
    recv_h,
):
    band = 2 * half
    rows, cols = theta_ref.shape
    stripe_rows = rows * groups
    wide = cols * cores
    kernels = row_taps_ref.shape[1]
    taps = row_taps_ref.shape[2]
    slots = cond_ref.shape[0] // cores
    stripe = lax.axis_index("stripe")
    group = lax.axis_index("cond")
    core = lax.axis_index("col")
    has_up = stripe > 0
    has_down = stripe < stripes - 1
    upper = half // rows
    in_upper = group < upper
    side = jnp.where(in_upper, -1, 1)
    has_side = jnp.where(in_upper, has_up, has_down)
    place = group * cores + core

    def peer(group_step, core_step):
        return {
            "stripe": stripe,
            "cond": lax.rem(group + group_step, groups),
            "col": lax.rem(core + core_step, cores),
        }

    def beside(step, to_group, to_core):
        return {"stripe": stripe + step, "cond": to_group, "col": to_core}

    everyone = [(g, c) for g in range(groups) for c in range(cores)]
    others = everyone[1:]
    lower_half = [(g, c) for g, c in everyone if g >= upper]
    upper_half = [(g, c) for g, c in everyone if g < upper]

    pairs = (
        (theta_in, theta_ref),
        (seed_in, seed_ref),
        (target_in, target_ref),
        (row_taps_in, row_taps_ref),
        (col_taps_in, col_taps_ref),
        (weight_in, weight_ref),
        (cond_in, cond_ref),
        (dose_in, dose_ref),
    )
    loads = [
        pltpu.make_async_copy(source, into, load_sem.at[i])
        for i, (source, into) in enumerate(pairs)
    ]
    for load in loads:
        load.start()

    barrier = pltpu.get_barrier_semaphore()

    def greet(device):
        pl.semaphore_signal(
            barrier, inc=1, device_id=device, device_id_type=pl.DeviceIdType.MESH
        )

    for group_step, core_step in others:
        greet(peer(group_step, core_step))
    for to_group, to_core in everyone:
        @pl.when(has_up & (in_upper if to_group < upper else True))
        def _(g=to_group, c=to_core):
            greet(beside(-1, g, c))

        @pl.when(has_down & (True if to_group < upper else jnp.logical_not(in_upper)))
        def _(g=to_group, c=to_core):
            greet(beside(1, g, c))

    loads[0].wait()
    loads[1].wait()
    sig = sigmoid(theta_ref[...] + seed_shift * (2 * seed_ref[...] - 1).astype(f32))
    sig_ref[...] = sig

    own_first = pl.multiple_of(half + group * rows, rows)
    own_left = pl.multiple_of(core * cols, cols)
    own_tile = ext.at[pl.ds(own_first, rows), pl.ds(own_left, cols)]
    ext[pl.ds(own_first, rows), pl.ds(own_left, cols)] = sig.astype(bf16)

    full, part = groups * cores, upper * cores
    near = jnp.where(has_up, jnp.where(in_upper, full, part), 0) + jnp.where(
        has_down, jnp.where(in_upper, part, full), 0
    )
    pl.semaphore_wait(barrier, full - 1 + near)

    def remote(source, target, send, recv, device):
        return pltpu.make_async_remote_copy(
            src_ref=source,
            dst_ref=target,
            send_sem=send,
            recv_sem=recv,
            device_id=device,
            device_id_type=pl.DeviceIdType.MESH,
        )

    far_first = jnp.where(
        in_upper, half + stripe_rows + group * rows, (group - upper) * rows
    )
    far_tile = ext.at[pl.ds(pl.multiple_of(far_first, rows), rows), pl.ds(own_left, cols)]

    def mask_far(to_group, to_core):
        at = to_group * cores + to_core
        return remote(
            own_tile,
            far_tile,
            send_f.at[at],
            recv_f.at[place],
            beside(side, to_group, to_core),
        )

    def mask_far_arrival(from_group, from_core):
        first = from_group * rows + (half + stripe_rows if from_group < upper else -half)
        tile = ext.at[first : first + rows, from_core * cols : (from_core + 1) * cols]
        at = from_group * cores + from_core
        return remote(tile, tile, send_f.at[at], recv_f.at[at], peer(0, 1))

    def mask_near(group_step, core_step):
        at = group_step * cores + core_step - 1
        return remote(
            own_tile, own_tile, send_m.at[at], recv_m.at[at], peer(group_step, core_step)
        )

    def mask_near_arrival(group_step, core_step):
        at = group_step * cores + core_step - 1
        from_group = lax.rem(group - group_step + groups, groups)
        from_core = lax.rem(core - core_step + cores, cores)
        tile = ext.at[
            pl.ds(pl.multiple_of(half + from_group * rows, rows), rows),
            pl.ds(pl.multiple_of(from_core * cols, cols), cols),
        ]
        return remote(tile, tile, send_m.at[at], recv_m.at[at], peer(group_step, core_step))

    @pl.when(has_side)
    def _():
        for to_group, to_core in everyone:
            mask_far(to_group, to_core).start()

    for group_step, core_step in reversed(others):
        mask_near(group_step, core_step).start()
    loads[2].wait()

    def target_copy(core_step):
        tile = tgt.at[:, pl.ds(own_left, cols)]
        return remote(
            target_ref, tile, send_t.at[core_step - 1], recv_t.at[core_step - 1], peer(0, core_step)
        )

    def target_arrival(core_step):
        from_core = lax.rem(core - core_step + cores, cores)
        tile = tgt.at[:, pl.ds(pl.multiple_of(from_core * cols, cols), cols)]
        return remote(
            tile, tile, send_t.at[core_step - 1], recv_t.at[core_step - 1], peer(0, core_step)
        )

    for core_step in range(1, cores):
        target_copy(core_step).start()
    tgt[:, pl.ds(own_left, cols)] = target_ref[...]

    @pl.when(jnp.logical_not(has_up))
    def _():
        ext[0:half, :] = jnp.zeros((half, wide), bf16)

    @pl.when(jnp.logical_not(has_down))
    def _():
        ext[half + stripe_rows :, :] = jnp.zeros((half, wide), bf16)

    taps_pad[...] = jnp.zeros_like(taps_pad)
    mirror = (
        lax.broadcasted_iota(jnp.int32, (2 * band, 3 * band), 0)
        + lax.broadcasted_iota(jnp.int32, (2 * band, 3 * band), 1)
        == band
    ).astype(f32).astype(bf16)

    for load in loads[3:]:
        load.wait()

    for slot in range(slots):
        focus = cond_ref[core * slots + slot]
        dose = dose_ref[core * slots + slot]

        taps_pad[0, 0:kernels, 0:taps] = row_taps_ref[focus].astype(f32)
        taps_pad[1, 0:kernels, 0:taps] = col_taps_ref[focus].astype(f32)
        for which in range(2):
            taps_pad[2 + which] = jnp.dot(
                taps_pad[which, :, 0 : 2 * band].astype(bf16),
                mirror,
                preferred_element_type=f32,
            )
        for k in range(kernels):
            tile = pl.ds(k * band, band)
            fwd_rows[tile, :] = toeplitz(taps_pad[0, k : k + 1, 0 : 2 * band], band, 0).astype(bf16)
            adjoint = toeplitz(taps_pad[2, k : k + 1, 0 : 2 * band], band, 0).astype(bf16)
            adj_rows[0:band, tile] = adjoint[:, band:]
            adj_rows[band:, tile] = adjoint[:, :band]
            for matrix, which in ((fwd_cols, 3), (adj_cols, 1)):
                strip = toeplitz(taps_pad[which, k : k + 1, :], band, half).astype(bf16)
                matrix[k, 0:band, 0:band] = strip[:, 2 * band :]
                matrix[k, 0:band, band:] = jnp.zeros((band, band), bf16)
                matrix[k, band : 2 * band, :] = strip[:, band:]
                matrix[k, 2 * band : 3 * band, :] = strip[:, : 2 * band]
                matrix[k, 3 * band :, 0:band] = jnp.zeros((band, band), bf16)
                matrix[k, 3 * band :, band:] = strip[:, 0:band]

        if slot == 0:
            for group_step, core_step in others:
                mask_near_arrival(group_step, core_step).wait_recv()

            @pl.when(has_up)
            def _():
                for from_group, from_core in lower_half:
                    mask_far_arrival(from_group, from_core).wait_recv()

            @pl.when(has_down)
            def _():
                for from_group, from_core in upper_half:
                    mask_far_arrival(from_group, from_core).wait_recv()

        def banded(left_side, matrix):
            pieces = []
            for first in range(0, wide, 2 * band):
                low = max(first - band, 0)
                high = min(first + 3 * band, wide)
                top = low - (first - band)
                pieces.append(
                    jnp.dot(
                        left_side[:, low:high],
                        matrix[top : top + high - low, :],
                        preferred_element_type=f32,
                    )
                )
            return jnp.concatenate(pieces, axis=1)

        row_pass[...] = jnp.dot(
            fwd_rows[...], ext[...], preferred_element_type=f32
        ).astype(bf16)
        intensity = jnp.zeros((band, wide), f32)
        for k in range(kernels):
            amp = banded(row_pass[k * band : (k + 1) * band, :], fwd_cols[k])
            field[k] = amp
            intensity = intensity + weight_ref[focus, k] * (amp * amp)
        if slot == 0:
            for core_step in range(1, cores):
                target_arrival(core_step).wait_recv()
        resist = sigmoid(steepness * (dose * intensity - threshold))
        aim = tgt[...].astype(f32)
        slope = (2.0 * steepness) * (resist - aim) * dose * resist * (1.0 - resist)
        for k in range(kernels):
            dfield = ((2.0 * weight_ref[focus, k]) * field[k] * slope).astype(bf16)
            col_back[k * band : (k + 1) * band, :] = banded(dfield, adj_cols[k]).astype(bf16)
        total = jnp.dot(adj_rows[...], col_back[...], preferred_element_type=f32)
        if slot == 0:
            grad[...] = total
        else:
            grad[...] += total

    grad_half[...] = grad[...].astype(bf16)

    def grad_near(group_step, core_step):
        to = peer(group_step, core_step)
        at = group_step * cores + core_step - 1
        return remote(
            grad_half.at[
                pl.ds(pl.multiple_of(half + to["cond"] * rows, rows), rows),
                pl.ds(pl.multiple_of(to["col"] * cols, cols), cols),
            ],
            partial.at[at],
            send_g.at[at],
            recv_g.at[at],
            to,
        )

    def grad_far(to_group, to_core):
        first = to_group * rows + (half + stripe_rows if to_group < upper else -half)
        at = to_group * cores + to_core
        return remote(
            grad_half.at[first : first + rows, to_core * cols : (to_core + 1) * cols],
            partial_far.at[place],
            send_h.at[at],
            recv_h.at[place],
            beside(1 if to_group < upper else -1, to_group, to_core),
        )

    def grad_far_arrival(from_group, from_core):
        at = from_group * cores + from_core
        tile = partial_far.at[at]
        return remote(tile, tile, send_h.at[at], recv_h.at[at], peer(0, 1))

    @pl.when(has_up)
    def _():
        for to_group, to_core in lower_half:
            grad_far(to_group, to_core).start()

    @pl.when(has_down)
    def _():
        for to_group, to_core in upper_half:
            grad_far(to_group, to_core).start()

    for group_step, core_step in reversed(others):
        grad_near(group_step, core_step).start()
    mine = grad[pl.ds(own_first, rows), pl.ds(own_left, cols)]
    for group_step, core_step in others:
        grad_near(group_step, core_step).wait_recv()
        mine = mine + partial[group_step * cores + core_step - 1].astype(f32)
    total_ref[...] = mine

    @pl.when(has_side)
    def _():
        more = jnp.zeros((rows, cols), f32)
        for from_group, from_core in everyone:
            grad_far_arrival(from_group, from_core).wait_recv()
            more = more + partial_far[from_group * cores + from_core].astype(f32)
        total_ref[...] += more

    sig = sig_ref[...]
    out_ref[...] = total_ref[...] * sig * (1.0 - sig)

    @pl.when(has_side)
    def _():
        for to_group, to_core in everyone:
            mask_far(to_group, to_core).wait_send()

    @pl.when(has_up)
    def _():
        for to_group, to_core in lower_half:
            grad_far(to_group, to_core).wait_send()

    @pl.when(has_down)
    def _():
        for to_group, to_core in upper_half:
            grad_far(to_group, to_core).wait_send()

    for group_step, core_step in others:
        mask_near(group_step, core_step).wait_send()
        grad_near(group_step, core_step).wait_send()
    for core_step in range(1, cores):
        target_copy(core_step).wait_send()


def shards(stripes, groups, cores, theta, seed_map, target, row_taps, col_taps, weight, cond_index, dose):
    rows, cols = theta.shape
    kernels, taps = row_taps.shape[1:]
    half = taps // 2
    band = 2 * half
    stripe_rows = rows * groups
    wide = cols * cores
    tall = stripe_rows + band
    vmem = pl.BlockSpec(memory_space=pltpu.VMEM)
    hbm = pl.BlockSpec(memory_space=pltpu.HBM)
    dma = pltpu.SemaphoreType.DMA
    peers = groups * cores - 1
    return pl.pallas_call(
        functools.partial(body, stripes, groups, cores, half),
        out_shape=jax.ShapeDtypeStruct((rows, cols), f32),
        in_specs=[hbm] * 8,
        out_specs=vmem,
        scratch_shapes=[
            *[pltpu.VMEM(a.shape, a.dtype) for a in (theta, seed_map, target, row_taps, col_taps)],
            *[pltpu.SMEM(a.shape, a.dtype) for a in (weight, cond_index, dose)],
            dma((8,)),
            pltpu.VMEM((tall, wide), bf16),
            pltpu.VMEM((stripe_rows, wide), bf16),
            pltpu.VMEM((rows, cols), f32),
            pltpu.VMEM((4, 8, 3 * band), f32),
            pltpu.VMEM((kernels * band, 2 * band), bf16),
            pltpu.VMEM((2 * band, kernels * band), bf16),
            pltpu.VMEM((kernels, 4 * band, 2 * band), bf16),
            pltpu.VMEM((kernels, 4 * band, 2 * band), bf16),
            pltpu.VMEM((kernels * band, wide), bf16),
            pltpu.VMEM((kernels, band, wide), f32),
            pltpu.VMEM((kernels * band, wide), bf16),
            pltpu.VMEM((tall, wide), f32),
            pltpu.VMEM((tall, wide), bf16),
            pltpu.VMEM((peers, rows, cols), bf16),
            pltpu.VMEM((peers + 1, rows, cols), bf16),
            pltpu.VMEM((rows, cols), f32),
            dma((peers,)),
            dma((peers,)),
            dma((peers + 1,)),
            dma((peers + 1,)),
            dma((cores - 1,)),
            dma((cores - 1,)),
            dma((peers,)),
            dma((peers,)),
            dma((peers + 1,)),
            dma((peers + 1,)),
        ],
        compiler_params=pltpu.CompilerParams(
            collective_id=0, has_side_effects=True, vmem_limit_bytes=40 * 1024 * 1024
        ),
    )(
        *[
            pltpu.with_memory_space_constraint(a, pltpu.HBM)
            for a in (theta, seed_map, target, row_taps, col_taps, weight, cond_index, dose)
        ]
    )


def solution(mesh):
    sizes = [mesh.shape[name] for name in ("stripe", "cond", "col")]
    return jax.shard_map(
        functools.partial(shards, *sizes),
        mesh=mesh,
        in_specs=(
            P(("blocks", "stripe", "cond"), "col"),
            P(("blocks", "stripe", "cond"), "col"),
            P(("blocks", "stripe"), "col"),
            P(),
            P(),
            P(),
            P("cond"),
            P("cond"),
        ),
        out_specs=P(("blocks", "stripe", "cond"), "col"),
        check_vma=False,
    )
```

```python
import functools

import jax
import jax.numpy as jnp
from jax import lax
from jax.experimental import pallas as pl
from jax.experimental.pallas import tpu as pltpu
from jax.sharding import PartitionSpec as P

seed_shift = 1.5
steepness = 4.0
threshold = 0.3
f32 = jnp.float32
bf16 = jnp.bfloat16


def sigmoid(x):
    return 1.0 / (1.0 + jnp.exp(-x))


def toeplitz(row, count, shift):
    wide = jnp.broadcast_to(row, (count, row.shape[1]))
    return pltpu.roll(wide, shift, 1, stride=1, stride_axis=0)


def body(
    stripes,
    groups,
    cores,
    half,
    theta_in,
    seed_in,
    target_in,
    row_taps_in,
    col_taps_in,
    weight_in,
    cond_in,
    dose_in,
    out_ref,
    theta_ref,
    seed_ref,
    target_ref,
    row_taps_ref,
    col_taps_ref,
    weight_ref,
    cond_ref,
    dose_ref,
    load_sem,
    ext,
    tgt,
    sig_ref,
    taps_pad,
    fwd_rows,
    adj_rows,
    fwd_cols,
    adj_cols,
    row_pass,
    field,
    col_back,
    grad,
    grad_half,
    partial,
    partial_far,
    total_ref,
    send_m,
    recv_m,
    send_f,
    recv_f,
    send_t,
    recv_t,
    send_g,
    recv_g,
    send_h,
    recv_h,
    send_r,
):
    band = 2 * half
    rows, cols = theta_ref.shape
    stripe_rows = rows * groups
    wide = cols * cores
    kernels = row_taps_ref.shape[1]
    taps = row_taps_ref.shape[2]
    slots = cond_ref.shape[0] // cores
    stripe = lax.axis_index("stripe")
    group = lax.axis_index("cond")
    core = lax.axis_index("col")
    has_up = stripe > 0
    has_down = stripe < stripes - 1
    upper = half // rows
    in_upper = group < upper
    side = jnp.where(in_upper, -1, 1)
    has_side = jnp.where(in_upper, has_up, has_down)
    place = group * cores + core

    def peer(group_step, core_step):
        return {
            "stripe": stripe,
            "cond": lax.rem(group + group_step, groups),
            "col": lax.rem(core + core_step, cores),
        }

    def beside(step, to_group, to_core):
        return {"stripe": stripe + step, "cond": to_group, "col": to_core}

    everyone = [(g, c) for g in range(groups) for c in range(cores)]
    others = everyone[1:]
    lower_half = [(g, c) for g, c in everyone if g >= upper]
    upper_half = [(g, c) for g, c in everyone if g < upper]

    pairs = (
        (theta_in, theta_ref),
        (seed_in, seed_ref),
        (target_in, target_ref),
        (row_taps_in, row_taps_ref),
        (col_taps_in, col_taps_ref),
        (weight_in, weight_ref),
        (cond_in, cond_ref),
        (dose_in, dose_ref),
    )
    loads = [
        pltpu.make_async_copy(source, into, load_sem.at[i])
        for i, (source, into) in enumerate(pairs)
    ]
    for load in loads:
        load.start()

    barrier = pltpu.get_barrier_semaphore()

    def greet(device):
        pl.semaphore_signal(
            barrier, inc=1, device_id=device, device_id_type=pl.DeviceIdType.MESH
        )

    for group_step, core_step in others:
        greet(peer(group_step, core_step))
    for to_group, to_core in everyone:
        @pl.when(has_up & (in_upper if to_group < upper else True))
        def _(g=to_group, c=to_core):
            greet(beside(-1, g, c))

        @pl.when(has_down & (True if to_group < upper else jnp.logical_not(in_upper)))
        def _(g=to_group, c=to_core):
            greet(beside(1, g, c))

    loads[0].wait()
    loads[1].wait()
    sig = sigmoid(theta_ref[...] + seed_shift * (2 * seed_ref[...] - 1).astype(f32))
    sig_ref[...] = sig

    own_first = pl.multiple_of(half + group * rows, rows)
    own_left = pl.multiple_of(core * cols, cols)
    own_tile = ext.at[pl.ds(own_first, rows), pl.ds(own_left, cols)]
    ext[pl.ds(own_first, rows), pl.ds(own_left, cols)] = sig.astype(bf16)

    full, part = groups * cores, upper * cores
    near = jnp.where(has_up, jnp.where(in_upper, full, part), 0) + jnp.where(
        has_down, jnp.where(in_upper, part, full), 0
    )
    pl.semaphore_wait(barrier, full - 1 + near)

    def remote(source, target, send, recv, device):
        return pltpu.make_async_remote_copy(
            src_ref=source,
            dst_ref=target,
            send_sem=send,
            recv_sem=recv,
            device_id=device,
            device_id_type=pl.DeviceIdType.MESH,
        )

    far_first = jnp.where(
        in_upper, half + stripe_rows + group * rows, (group - upper) * rows
    )
    far_tile = ext.at[pl.ds(pl.multiple_of(far_first, rows), rows), pl.ds(own_left, cols)]

    far_steps = [(g, 0) for g in range(1, groups)] + [(0, c) for c in range(cores)]

    def mask_far(group_step, core_step):
        at = group_step * cores + core_step
        near_side = peer(group_step, core_step)
        return remote(
            own_tile,
            far_tile,
            send_f.at[at],
            recv_f.at[place],
            beside(side, near_side["cond"], near_side["col"]),
        )

    def relay(from_group):
        first = from_group * rows + (half + stripe_rows if from_group < upper else -half)
        tile = ext.at[first : first + rows, pl.ds(own_left, cols)]
        at = from_group * cores + core
        return remote(tile, tile, send_r.at[from_group], recv_f.at[at], peer(0, 1))

    def mask_far_arrival(from_group, from_core):
        first = from_group * rows + (half + stripe_rows if from_group < upper else -half)
        tile = ext.at[first : first + rows, from_core * cols : (from_core + 1) * cols]
        at = from_group * cores + from_core
        return remote(tile, tile, send_f.at[at], recv_f.at[at], peer(0, 1))

    def mask_near(group_step, core_step):
        at = group_step * cores + core_step - 1
        return remote(
            own_tile, own_tile, send_m.at[at], recv_m.at[at], peer(group_step, core_step)
        )

    def mask_near_arrival(group_step, core_step):
        at = group_step * cores + core_step - 1
        from_group = lax.rem(group - group_step + groups, groups)
        from_core = lax.rem(core - core_step + cores, cores)
        tile = ext.at[
            pl.ds(pl.multiple_of(half + from_group * rows, rows), rows),
            pl.ds(pl.multiple_of(from_core * cols, cols), cols),
        ]
        return remote(tile, tile, send_m.at[at], recv_m.at[at], peer(group_step, core_step))

    @pl.when(has_side)
    def _():
        for group_step, core_step in far_steps:
            mask_far(group_step, core_step).start()

    for group_step, core_step in reversed(others):
        mask_near(group_step, core_step).start()
    loads[2].wait()

    def target_copy(core_step):
        tile = tgt.at[:, pl.ds(own_left, cols)]
        return remote(
            target_ref, tile, send_t.at[core_step - 1], recv_t.at[core_step - 1], peer(0, core_step)
        )

    def target_arrival(core_step):
        from_core = lax.rem(core - core_step + cores, cores)
        tile = tgt.at[:, pl.ds(pl.multiple_of(from_core * cols, cols), cols)]
        return remote(
            tile, tile, send_t.at[core_step - 1], recv_t.at[core_step - 1], peer(0, core_step)
        )

    for core_step in range(1, cores):
        target_copy(core_step).start()
    tgt[:, pl.ds(own_left, cols)] = target_ref[...]

    @pl.when(jnp.logical_not(has_up))
    def _():
        ext[0:half, :] = jnp.zeros((half, wide), bf16)

    @pl.when(jnp.logical_not(has_down))
    def _():
        ext[half + stripe_rows :, :] = jnp.zeros((half, wide), bf16)

    taps_pad[...] = jnp.zeros_like(taps_pad)
    mirror = (
        lax.broadcasted_iota(jnp.int32, (2 * band, 3 * band), 0)
        + lax.broadcasted_iota(jnp.int32, (2 * band, 3 * band), 1)
        == band
    ).astype(f32).astype(bf16)

    for load in loads[3:]:
        load.wait()

    for slot in range(slots):
        focus = cond_ref[core * slots + slot]
        dose = dose_ref[core * slots + slot]

        taps_pad[0, 0:kernels, 0:taps] = row_taps_ref[focus].astype(f32)
        taps_pad[1, 0:kernels, 0:taps] = col_taps_ref[focus].astype(f32)
        for which in range(2):
            taps_pad[2 + which] = jnp.dot(
                taps_pad[which, :, 0 : 2 * band].astype(bf16),
                mirror,
                preferred_element_type=f32,
            )
        for k in range(kernels):
            tile = pl.ds(k * band, band)
            fwd_rows[tile, :] = toeplitz(taps_pad[0, k : k + 1, 0 : 2 * band], band, 0).astype(bf16)
            adjoint = toeplitz(taps_pad[2, k : k + 1, 0 : 2 * band], band, 0).astype(bf16)
            adj_rows[0:band, tile] = adjoint[:, band:]
            adj_rows[band:, tile] = adjoint[:, :band]
            for matrix, which in ((fwd_cols, 3), (adj_cols, 1)):
                strip = toeplitz(taps_pad[which, k : k + 1, :], band, half).astype(bf16)
                matrix[k, 0:band, 0:band] = strip[:, 2 * band :]
                matrix[k, 0:band, band:] = jnp.zeros((band, band), bf16)
                matrix[k, band : 2 * band, :] = strip[:, band:]
                matrix[k, 2 * band : 3 * band, :] = strip[:, : 2 * band]
                matrix[k, 3 * band :, 0:band] = jnp.zeros((band, band), bf16)
                matrix[k, 3 * band :, band:] = strip[:, 0:band]

        if slot == 0:
            for from_group in range(groups):

                @pl.when((has_down if from_group < upper else has_up) & (group != from_group))
                def _(g=from_group):
                    relay(g).wait_recv()
                    relay(g).start()

            for group_step, core_step in others:
                mask_near_arrival(group_step, core_step).wait_recv()
            for from_group, from_core in everyone:

                @pl.when(
                    (has_down if from_group < upper else has_up)
                    & ((group == from_group) | (core != from_core))
                )
                def _(g=from_group, c=from_core):
                    mask_far_arrival(g, c).wait_recv()

        def banded(left_side, matrix):
            pieces = []
            for first in range(0, wide, 2 * band):
                low = max(first - band, 0)
                high = min(first + 3 * band, wide)
                top = low - (first - band)
                pieces.append(
                    jnp.dot(
                        left_side[:, low:high],
                        matrix[top : top + high - low, :],
                        preferred_element_type=f32,
                    )
                )
            return jnp.concatenate(pieces, axis=1)

        row_pass[...] = jnp.dot(
            fwd_rows[...], ext[...], preferred_element_type=f32
        ).astype(bf16)
        intensity = jnp.zeros((band, wide), f32)
        for k in range(kernels):
            amp = banded(row_pass[k * band : (k + 1) * band, :], fwd_cols[k])
            field[k] = amp
            intensity = intensity + weight_ref[focus, k] * (amp * amp)
        if slot == 0:
            for core_step in range(1, cores):
                target_arrival(core_step).wait_recv()
        resist = sigmoid(steepness * (dose * intensity - threshold))
        aim = tgt[...].astype(f32)
        slope = (2.0 * steepness) * (resist - aim) * dose * resist * (1.0 - resist)
        for k in range(kernels):
            dfield = ((2.0 * weight_ref[focus, k]) * field[k] * slope).astype(bf16)
            col_back[k * band : (k + 1) * band, :] = banded(dfield, adj_cols[k]).astype(bf16)
        total = jnp.dot(adj_rows[...], col_back[...], preferred_element_type=f32)
        if slot == 0:
            grad[...] = total
        else:
            grad[...] += total

    grad_half[...] = grad[...].astype(bf16)

    def grad_near(group_step, core_step):
        to = peer(group_step, core_step)
        at = group_step * cores + core_step - 1
        return remote(
            grad_half.at[
                pl.ds(pl.multiple_of(half + to["cond"] * rows, rows), rows),
                pl.ds(pl.multiple_of(to["col"] * cols, cols), cols),
            ],
            partial.at[at],
            send_g.at[at],
            recv_g.at[at],
            to,
        )

    def grad_far(to_group, to_core):
        first = to_group * rows + (half + stripe_rows if to_group < upper else -half)
        at = to_group * cores + to_core
        return remote(
            grad_half.at[first : first + rows, to_core * cols : (to_core + 1) * cols],
            partial_far.at[place],
            send_h.at[at],
            recv_h.at[place],
            beside(1 if to_group < upper else -1, to_group, to_core),
        )

    def grad_far_arrival(from_group, from_core):
        at = from_group * cores + from_core
        tile = partial_far.at[at]
        return remote(tile, tile, send_h.at[at], recv_h.at[at], peer(0, 1))

    @pl.when(has_up)
    def _():
        for to_group, to_core in lower_half:
            grad_far(to_group, to_core).start()

    @pl.when(has_down)
    def _():
        for to_group, to_core in upper_half:
            grad_far(to_group, to_core).start()

    for group_step, core_step in reversed(others):
        grad_near(group_step, core_step).start()
    mine = grad[pl.ds(own_first, rows), pl.ds(own_left, cols)]
    for group_step, core_step in others:
        grad_near(group_step, core_step).wait_recv()
        mine = mine + partial[group_step * cores + core_step - 1].astype(f32)
    total_ref[...] = mine

    @pl.when(has_side)
    def _():
        more = jnp.zeros((rows, cols), f32)
        for from_group, from_core in everyone:
            grad_far_arrival(from_group, from_core).wait_recv()
            more = more + partial_far[from_group * cores + from_core].astype(f32)
        total_ref[...] += more

    sig = sig_ref[...]
    out_ref[...] = total_ref[...] * sig * (1.0 - sig)

    @pl.when(has_side)
    def _():
        for group_step, core_step in far_steps:
            mask_far(group_step, core_step).wait_send()

    @pl.when(has_up)
    def _():
        for to_group, to_core in lower_half:
            grad_far(to_group, to_core).wait_send()

    @pl.when(has_down)
    def _():
        for to_group, to_core in upper_half:
            grad_far(to_group, to_core).wait_send()

    for group_step, core_step in others:
        mask_near(group_step, core_step).wait_send()
        grad_near(group_step, core_step).wait_send()
    for core_step in range(1, cores):
        target_copy(core_step).wait_send()
    for from_group in range(groups):
        @pl.when((has_down if from_group < upper else has_up) & (group != from_group))
        def _(g=from_group):
            relay(g).wait_send()


def shards(stripes, groups, cores, theta, seed_map, target, row_taps, col_taps, weight, cond_index, dose):
    rows, cols = theta.shape
    kernels, taps = row_taps.shape[1:]
    half = taps // 2
    band = 2 * half
    stripe_rows = rows * groups
    wide = cols * cores
    tall = stripe_rows + band
    vmem = pl.BlockSpec(memory_space=pltpu.VMEM)
    hbm = pl.BlockSpec(memory_space=pltpu.HBM)
    dma = pltpu.SemaphoreType.DMA
    peers = groups * cores - 1
    return pl.pallas_call(
        functools.partial(body, stripes, groups, cores, half),
        out_shape=jax.ShapeDtypeStruct((rows, cols), f32),
        in_specs=[hbm] * 8,
        out_specs=vmem,
        scratch_shapes=[
            *[pltpu.VMEM(a.shape, a.dtype) for a in (theta, seed_map, target, row_taps, col_taps)],
            *[pltpu.SMEM(a.shape, a.dtype) for a in (weight, cond_index, dose)],
            dma((8,)),
            pltpu.VMEM((tall, wide), bf16),
            pltpu.VMEM((stripe_rows, wide), bf16),
            pltpu.VMEM((rows, cols), f32),
            pltpu.VMEM((4, 8, 3 * band), f32),
            pltpu.VMEM((kernels * band, 2 * band), bf16),
            pltpu.VMEM((2 * band, kernels * band), bf16),
            pltpu.VMEM((kernels, 4 * band, 2 * band), bf16),
            pltpu.VMEM((kernels, 4 * band, 2 * band), bf16),
            pltpu.VMEM((kernels * band, wide), bf16),
            pltpu.VMEM((kernels, band, wide), f32),
            pltpu.VMEM((kernels * band, wide), bf16),
            pltpu.VMEM((tall, wide), f32),
            pltpu.VMEM((tall, wide), bf16),
            pltpu.VMEM((peers, rows, cols), bf16),
            pltpu.VMEM((peers + 1, rows, cols), bf16),
            pltpu.VMEM((rows, cols), f32),
            dma((peers,)),
            dma((peers,)),
            dma((peers + 1,)),
            dma((peers + 1,)),
            dma((cores - 1,)),
            dma((cores - 1,)),
            dma((peers,)),
            dma((peers,)),
            dma((peers + 1,)),
            dma((peers + 1,)),
            dma((groups,)),
        ],
        compiler_params=pltpu.CompilerParams(
            collective_id=0, has_side_effects=True, vmem_limit_bytes=40 * 1024 * 1024
        ),
    )(
        *[
            pltpu.with_memory_space_constraint(a, pltpu.HBM)
            for a in (theta, seed_map, target, row_taps, col_taps, weight, cond_index, dose)
        ]
    )


def solution(mesh):
    sizes = [mesh.shape[name] for name in ("stripe", "cond", "col")]
    return jax.shard_map(
        functools.partial(shards, *sizes),
        mesh=mesh,
        in_specs=(
            P(("blocks", "stripe", "cond"), "col"),
            P(("blocks", "stripe", "cond"), "col"),
            P(("blocks", "stripe"), "col"),
            P(),
            P(),
            P(),
            P("cond"),
            P("cond"),
        ),
        out_specs=P(("blocks", "stripe", "cond"), "col"),
        check_vma=False,
    )
```

```python
import functools

import jax
import jax.numpy as jnp
from jax import lax
from jax.experimental import pallas as pl
from jax.experimental.pallas import tpu as pltpu
from jax.sharding import PartitionSpec as P

seed_shift = 1.5
steepness = 4.0
threshold = 0.3
f32 = jnp.float32
bf16 = jnp.bfloat16


def sigmoid(x):
    return 1.0 / (1.0 + jnp.exp(-x))


def toeplitz(row, count, shift):
    wide = jnp.broadcast_to(row, (count, row.shape[1]))
    return pltpu.roll(wide, shift, 1, stride=1, stride_axis=0)


def body(
    stripes,
    groups,
    cores,
    half,
    theta_in,
    seed_in,
    target_in,
    row_taps_in,
    col_taps_in,
    weight_in,
    cond_in,
    dose_in,
    out_ref,
    theta_ref,
    seed_ref,
    target_ref,
    row_taps_ref,
    col_taps_ref,
    weight_ref,
    cond_ref,
    dose_ref,
    load_sem,
    ext,
    tgt,
    sig_ref,
    taps_pad,
    fwd_rows,
    adj_rows,
    fwd_cols,
    adj_cols,
    row_pass,
    field,
    col_back,
    grad,
    grad_half,
    partial,
    partial_far,
    total_ref,
    send_m,
    recv_m,
    send_f,
    recv_f,
    send_t,
    recv_t,
    send_g,
    recv_g,
    send_h,
    recv_h,
    send_r,
):
    band = 2 * half
    rows, cols = theta_ref.shape
    stripe_rows = rows * groups
    wide = cols * cores
    kernels = row_taps_ref.shape[1]
    taps = row_taps_ref.shape[2]
    slots = cond_ref.shape[0] // cores
    stripe = lax.axis_index("stripe")
    group = lax.axis_index("cond")
    core = lax.axis_index("col")
    has_up = stripe > 0
    has_down = stripe < stripes - 1
    upper = half // rows
    in_upper = group < upper
    side = jnp.where(in_upper, -1, 1)
    has_side = jnp.where(in_upper, has_up, has_down)
    place = group * cores + core

    def peer(group_step, core_step):
        return {
            "stripe": stripe,
            "cond": lax.rem(group + group_step, groups),
            "col": lax.rem(core + core_step, cores),
        }

    def beside(step, to_group, to_core):
        return {"stripe": stripe + step, "cond": to_group, "col": to_core}

    everyone = [(g, c) for g in range(groups) for c in range(cores)]
    others = everyone[1:]
    lower_half = [(g, c) for g, c in everyone if g >= upper]
    upper_half = [(g, c) for g, c in everyone if g < upper]

    pairs = (
        (theta_in, theta_ref),
        (seed_in, seed_ref),
        (target_in, target_ref),
        (row_taps_in, row_taps_ref),
        (col_taps_in, col_taps_ref),
        (weight_in, weight_ref),
        (cond_in, cond_ref),
        (dose_in, dose_ref),
    )
    loads = [
        pltpu.make_async_copy(source, into, load_sem.at[i])
        for i, (source, into) in enumerate(pairs)
    ]
    for load in loads:
        load.start()

    barrier = pltpu.get_barrier_semaphore()

    def greet(device):
        pl.semaphore_signal(
            barrier, inc=1, device_id=device, device_id_type=pl.DeviceIdType.MESH
        )

    for group_step, core_step in others:
        greet(peer(group_step, core_step))
    for to_group, to_core in everyone:
        @pl.when(has_up & (in_upper if to_group < upper else True))
        def _(g=to_group, c=to_core):
            greet(beside(-1, g, c))

        @pl.when(has_down & (True if to_group < upper else jnp.logical_not(in_upper)))
        def _(g=to_group, c=to_core):
            greet(beside(1, g, c))

    loads[0].wait()
    loads[1].wait()
    sig = sigmoid(theta_ref[...] + seed_shift * (2 * seed_ref[...] - 1).astype(f32))
    sig_ref[...] = sig

    own_first = pl.multiple_of(half + group * rows, rows)
    own_left = pl.multiple_of(core * cols, cols)
    own_tile = ext.at[pl.ds(own_first, rows), pl.ds(own_left, cols)]
    ext[pl.ds(own_first, rows), pl.ds(own_left, cols)] = sig.astype(bf16)

    full, part = groups * cores, upper * cores
    near = jnp.where(has_up, jnp.where(in_upper, full, part), 0) + jnp.where(
        has_down, jnp.where(in_upper, part, full), 0
    )
    pl.semaphore_wait(barrier, full - 1 + near)

    def remote(source, target, send, recv, device):
        return pltpu.make_async_remote_copy(
            src_ref=source,
            dst_ref=target,
            send_sem=send,
            recv_sem=recv,
            device_id=device,
            device_id_type=pl.DeviceIdType.MESH,
        )

    far_first = jnp.where(
        in_upper, half + stripe_rows + group * rows, (group - upper) * rows
    )
    far_tile = ext.at[pl.ds(pl.multiple_of(far_first, rows), rows), pl.ds(own_left, cols)]

    far_steps = [(g, 0) for g in range(1, groups)] + [(0, c) for c in range(cores)]

    def mask_far(group_step, core_step):
        at = group_step * cores + core_step
        near_side = peer(group_step, core_step)
        return remote(
            own_tile,
            far_tile,
            send_f.at[at],
            recv_f.at[place],
            beside(side, near_side["cond"], near_side["col"]),
        )

    def relay(from_group):
        first = from_group * rows + (half + stripe_rows if from_group < upper else -half)
        tile = ext.at[first : first + rows, pl.ds(own_left, cols)]
        at = from_group * cores + core
        return remote(tile, tile, send_r.at[from_group], recv_f.at[at], peer(0, 1))

    def mask_far_arrival(from_group, from_core):
        first = from_group * rows + (half + stripe_rows if from_group < upper else -half)
        tile = ext.at[first : first + rows, from_core * cols : (from_core + 1) * cols]
        at = from_group * cores + from_core
        return remote(tile, tile, send_f.at[at], recv_f.at[at], peer(0, 1))

    def mask_near(group_step, core_step):
        at = group_step * cores + core_step - 1
        return remote(
            own_tile, own_tile, send_m.at[at], recv_m.at[at], peer(group_step, core_step)
        )

    def mask_near_arrival(group_step, core_step):
        at = group_step * cores + core_step - 1
        from_group = lax.rem(group - group_step + groups, groups)
        from_core = lax.rem(core - core_step + cores, cores)
        tile = ext.at[
            pl.ds(pl.multiple_of(half + from_group * rows, rows), rows),
            pl.ds(pl.multiple_of(from_core * cols, cols), cols),
        ]
        return remote(tile, tile, send_m.at[at], recv_m.at[at], peer(group_step, core_step))

    @pl.when(has_side)
    def _():
        for group_step, core_step in far_steps:
            mask_far(group_step, core_step).start()

    for group_step, core_step in reversed(others):
        mask_near(group_step, core_step).start()
    loads[2].wait()

    def target_copy(core_step):
        tile = tgt.at[:, pl.ds(own_left, cols)]
        return remote(
            target_ref, tile, send_t.at[core_step - 1], recv_t.at[core_step - 1], peer(0, core_step)
        )

    def target_arrival(core_step):
        from_core = lax.rem(core - core_step + cores, cores)
        tile = tgt.at[:, pl.ds(pl.multiple_of(from_core * cols, cols), cols)]
        return remote(
            tile, tile, send_t.at[core_step - 1], recv_t.at[core_step - 1], peer(0, core_step)
        )

    for core_step in range(1, cores):
        target_copy(core_step).start()
    tgt[:, pl.ds(own_left, cols)] = target_ref[...]

    @pl.when(jnp.logical_not(has_up))
    def _():
        ext[0:half, :] = jnp.zeros((half, wide), bf16)

    @pl.when(jnp.logical_not(has_down))
    def _():
        ext[half + stripe_rows :, :] = jnp.zeros((half, wide), bf16)

    taps_pad[...] = jnp.zeros_like(taps_pad)
    mirror = (
        lax.broadcasted_iota(jnp.int32, (2 * band, 3 * band), 0)
        + lax.broadcasted_iota(jnp.int32, (2 * band, 3 * band), 1)
        == band
    ).astype(f32).astype(bf16)

    for load in loads[3:]:
        load.wait()

    for slot in range(slots):
        focus = cond_ref[core * slots + slot]
        dose = dose_ref[core * slots + slot]

        taps_pad[0, 0:kernels, 0:taps] = row_taps_ref[focus].astype(f32)
        taps_pad[1, 0:kernels, 0:taps] = col_taps_ref[focus].astype(f32)
        for which in range(2):
            taps_pad[2 + which] = jnp.dot(
                taps_pad[which, :, 0 : 2 * band].astype(bf16),
                mirror,
                preferred_element_type=f32,
            )
        for k in range(kernels):
            tile = pl.ds(k * band, band)
            fwd_rows[tile, :] = toeplitz(taps_pad[0, k : k + 1, 0 : 2 * band], band, 0).astype(bf16)
            adjoint = toeplitz(taps_pad[2, k : k + 1, 0 : 2 * band], band, 0).astype(bf16)
            adj_rows[0:band, tile] = adjoint[:, band:]
            adj_rows[band:, tile] = adjoint[:, :band]
            for matrix, which in ((fwd_cols, 3), (adj_cols, 1)):
                strip = toeplitz(taps_pad[which, k : k + 1, :], band, half).astype(bf16)
                matrix[k, 0:band, 0:band] = strip[:, 2 * band :]
                matrix[k, 0:band, band:] = jnp.zeros((band, band), bf16)
                matrix[k, band : 2 * band, :] = strip[:, band:]
                matrix[k, 2 * band : 3 * band, :] = strip[:, : 2 * band]
                matrix[k, 3 * band :, 0:band] = jnp.zeros((band, band), bf16)
                matrix[k, 3 * band :, band:] = strip[:, 0:band]

        if slot == 0:
            for from_group in range(groups):

                @pl.when((has_down if from_group < upper else has_up) & (group != from_group))
                def _(g=from_group):
                    relay(g).wait_recv()
                    relay(g).start()

            for group_step, core_step in others:
                mask_near_arrival(group_step, core_step).wait_recv()
            for from_group, from_core in everyone:

                @pl.when(
                    (has_down if from_group < upper else has_up)
                    & ((group == from_group) | (core != from_core))
                )
                def _(g=from_group, c=from_core):
                    mask_far_arrival(g, c).wait_recv()

        def banded(left_side, matrix):
            pieces = []
            for first in range(0, wide, 2 * band):
                low = max(first - band, 0)
                high = min(first + 3 * band, wide)
                top = low - (first - band)
                pieces.append(
                    jnp.dot(
                        left_side[:, low:high],
                        matrix[top : top + high - low, :],
                        preferred_element_type=f32,
                    )
                )
            return jnp.concatenate(pieces, axis=1)

        row_pass[...] = jnp.dot(
            fwd_rows[...], ext[...], preferred_element_type=f32
        ).astype(bf16)
        intensity = jnp.zeros((band, wide), f32)
        for k in range(kernels):
            amp = banded(row_pass[k * band : (k + 1) * band, :], fwd_cols[k])
            field[k] = amp
            intensity = intensity + weight_ref[focus, k] * (amp * amp)
        if slot == 0:
            for core_step in range(1, cores):
                target_arrival(core_step).wait_recv()
        resist = sigmoid(steepness * (dose * intensity - threshold))
        aim = tgt[...].astype(f32)
        slope = (2.0 * steepness) * (resist - aim) * dose * resist * (1.0 - resist)
        for k in range(kernels):
            dfield = ((2.0 * weight_ref[focus, k]) * field[k] * slope).astype(bf16)
            col_back[k * band : (k + 1) * band, :] = banded(dfield, adj_cols[k]).astype(bf16)
        total = jnp.dot(adj_rows[...], col_back[...], preferred_element_type=f32)
        if slot == 0:
            grad[...] = total
        else:
            grad[...] += total

    grad_half[...] = grad[...].astype(bf16)

    def grad_near(group_step, core_step):
        to = peer(group_step, core_step)
        at = group_step * cores + core_step - 1
        return remote(
            grad_half.at[
                pl.ds(pl.multiple_of(half + to["cond"] * rows, rows), rows),
                pl.ds(pl.multiple_of(to["col"] * cols, cols), cols),
            ],
            partial.at[at],
            send_g.at[at],
            recv_g.at[at],
            to,
        )

    def grad_far(to_group, to_core):
        first = to_group * rows + (half + stripe_rows if to_group < upper else -half)
        at = to_group * cores + to_core
        return remote(
            grad_half.at[first : first + rows, to_core * cols : (to_core + 1) * cols],
            partial_far.at[place],
            send_h.at[at],
            recv_h.at[place],
            beside(1 if to_group < upper else -1, to_group, to_core),
        )

    def grad_far_arrival(from_group, from_core):
        at = from_group * cores + from_core
        tile = partial_far.at[at]
        return remote(tile, tile, send_h.at[at], recv_h.at[at], peer(0, 1))

    for group_step, core_step in reversed(others):
        grad_near(group_step, core_step).start()

    @pl.when(has_up)
    def _():
        for to_group, to_core in lower_half:
            grad_far(to_group, to_core).start()

    @pl.when(has_down)
    def _():
        for to_group, to_core in upper_half:
            grad_far(to_group, to_core).start()

    mine = grad[pl.ds(own_first, rows), pl.ds(own_left, cols)]
    for group_step, core_step in others:
        grad_near(group_step, core_step).wait_recv()
        mine = mine + partial[group_step * cores + core_step - 1].astype(f32)
    total_ref[...] = mine

    @pl.when(has_side)
    def _():
        more = jnp.zeros((rows, cols), f32)
        for from_group, from_core in everyone:
            grad_far_arrival(from_group, from_core).wait_recv()
            more = more + partial_far[from_group * cores + from_core].astype(f32)
        total_ref[...] += more

    sig = sig_ref[...]
    out_ref[...] = total_ref[...] * sig * (1.0 - sig)

    @pl.when(has_side)
    def _():
        for group_step, core_step in far_steps:
            mask_far(group_step, core_step).wait_send()

    @pl.when(has_up)
    def _():
        for to_group, to_core in lower_half:
            grad_far(to_group, to_core).wait_send()

    @pl.when(has_down)
    def _():
        for to_group, to_core in upper_half:
            grad_far(to_group, to_core).wait_send()

    for group_step, core_step in others:
        mask_near(group_step, core_step).wait_send()
        grad_near(group_step, core_step).wait_send()
    for core_step in range(1, cores):
        target_copy(core_step).wait_send()
    for from_group in range(groups):
        @pl.when((has_down if from_group < upper else has_up) & (group != from_group))
        def _(g=from_group):
            relay(g).wait_send()


def shards(stripes, groups, cores, theta, seed_map, target, row_taps, col_taps, weight, cond_index, dose):
    rows, cols = theta.shape
    kernels, taps = row_taps.shape[1:]
    half = taps // 2
    band = 2 * half
    stripe_rows = rows * groups
    wide = cols * cores
    tall = stripe_rows + band
    vmem = pl.BlockSpec(memory_space=pltpu.VMEM)
    hbm = pl.BlockSpec(memory_space=pltpu.HBM)
    dma = pltpu.SemaphoreType.DMA
    peers = groups * cores - 1
    return pl.pallas_call(
        functools.partial(body, stripes, groups, cores, half),
        out_shape=jax.ShapeDtypeStruct((rows, cols), f32),
        in_specs=[hbm] * 8,
        out_specs=vmem,
        scratch_shapes=[
            *[pltpu.VMEM(a.shape, a.dtype) for a in (theta, seed_map, target, row_taps, col_taps)],
            *[pltpu.SMEM(a.shape, a.dtype) for a in (weight, cond_index, dose)],
            dma((8,)),
            pltpu.VMEM((tall, wide), bf16),
            pltpu.VMEM((stripe_rows, wide), bf16),
            pltpu.VMEM((rows, cols), f32),
            pltpu.VMEM((4, 8, 3 * band), f32),
            pltpu.VMEM((kernels * band, 2 * band), bf16),
            pltpu.VMEM((2 * band, kernels * band), bf16),
            pltpu.VMEM((kernels, 4 * band, 2 * band), bf16),
            pltpu.VMEM((kernels, 4 * band, 2 * band), bf16),
            pltpu.VMEM((kernels * band, wide), bf16),
            pltpu.VMEM((kernels, band, wide), f32),
            pltpu.VMEM((kernels * band, wide), bf16),
            pltpu.VMEM((tall, wide), f32),
            pltpu.VMEM((tall, wide), bf16),
            pltpu.VMEM((peers, rows, cols), bf16),
            pltpu.VMEM((peers + 1, rows, cols), bf16),
            pltpu.VMEM((rows, cols), f32),
            dma((peers,)),
            dma((peers,)),
            dma((peers + 1,)),
            dma((peers + 1,)),
            dma((cores - 1,)),
            dma((cores - 1,)),
            dma((peers,)),
            dma((peers,)),
            dma((peers + 1,)),
            dma((peers + 1,)),
            dma((groups,)),
        ],
        compiler_params=pltpu.CompilerParams(
            collective_id=0, has_side_effects=True, vmem_limit_bytes=40 * 1024 * 1024
        ),
    )(
        *[
            pltpu.with_memory_space_constraint(a, pltpu.HBM)
            for a in (theta, seed_map, target, row_taps, col_taps, weight, cond_index, dose)
        ]
    )


def solution(mesh):
    sizes = [mesh.shape[name] for name in ("stripe", "cond", "col")]
    return jax.shard_map(
        functools.partial(shards, *sizes),
        mesh=mesh,
        in_specs=(
            P(("blocks", "stripe", "cond"), "col"),
            P(("blocks", "stripe", "cond"), "col"),
            P(("blocks", "stripe"), "col"),
            P(),
            P(),
            P(),
            P("cond"),
            P("cond"),
        ),
        out_specs=P(("blocks", "stripe", "cond"), "col"),
        check_vma=False,
    )
```
